768 devices in a mesh: mesh: 24 (over x, z_lo), harm: 32 (over y, z_hi, core).
Axes of the slice: x: 4, y: 8, z: 12 (z_hi: 2, z_lo: 6; z = z_hi * 6 + z_lo), core: 2. Of those that a mesh axis runs over, the one named last changes fastest.
Arguments:
- current_pattern: float32 [768, 4096], P('mesh'), may hold values from -6 to 6
- conductivity: float32 [768, 4096], P('mesh'), may hold values from 0.5 to 8
- cooling: float32 [768, 4096], P('mesh'), may hold values from 0.05 to 0.5
- harm_order: int32 [32], P('harm'), may hold values from 8 to 64
- harm_amp: int32 [32], P('harm'), may hold values from 1 to 4
- block_counts: int32 [32], P('harm'), may hold values from 1 to 32, as said below
Outputs:
- averaged_dissipation: float32 [768, 4096], P('mesh', 'harm')
- thermal_increase: float32 [768, 4096], P('mesh', 'harm')
The draws below stay inside these ranges and needn't reach their ends.
Inputs may be any that keep to these rules, and one draw needn't show every extreme that they name: `block_counts`: some harmonic has block count 32.
All inputs are finite; a program needn't handle non-finite values.
Results may differ from the reference program's by a relative error of at most 0.00002.
Values sent between devices are 32-bit elements; how exact they have to be, the bound alone decides.
A program may use at most 32 MiB of HBM per device.

```python
import math
import jax
import jax.numpy as jnp
from jax import lax

L = 4096
BLK = 128
EDDY_SWEEPS = 3
HEAT_SWEEPS = 4
NBLK = 32
HARMS = 32
NX = 768


def draw_block_counts(key, part):
    first, second = jax.random.split(jax.random.fold_in(key, 7))
    counts = jax.random.randint(first, (HARMS,), 1, NBLK + 1)
    where = jax.random.randint(second, (), 0, HARMS)
    return jnp.where(jnp.arange(HARMS) == where, NBLK, counts).astype(jnp.int32)


def with_ends(values, stream_key, low, largest):
    extent = values.shape
    place = [jax.random.randint(jax.random.fold_in(stream_key, axis), (), 0, extent[axis]) for axis in range(len(extent))]
    values = values.at[tuple(place)].set(low)
    longest = extent.index(max(extent))
    place[longest] = (place[longest] + 1) % extent[longest]
    return values.at[tuple(place)].set(largest)


def block_scale(key, extent, cuts, least, high):
    def one(dim, parts):
        heights = jax.random.uniform(jax.random.fold_in(jax.random.fold_in(key, 6), dim), (parts,), jnp.float32, least / len(cuts), high / len(cuts))
        return jnp.repeat(jnp.exp(heights), extent[dim] // parts).reshape((-1,) + (1,) * (len(extent) - dim - 1))

    gain = one(*cuts[0])
    for cut in cuts[1:]:
        gain = gain * one(*cut)
    return gain


def scatter_about(stream_key, shape, spread, limit, shards=(), held_as=jnp.bfloat16):
    entries = spread * jax.random.normal(stream_key, shape, jnp.float32)
    if shards:
        entries = entries * block_scale(stream_key, shape, shards, -0.22, 0.18)
    return jnp.clip(entries, -limit, limit).astype(held_as)


def setup_inputs(seed: int = 0) -> dict:
    streams_of = jax.random.split(jax.random.key(seed), 7)
    current_pattern = scatter_about(streams_of[0], (NX, L), 1.0, 6.0, ((0, 24),), jnp.float32)
    conductivity = jnp.clip(jnp.exp(math.log(8.0) - 2.7725887 * jax.random.uniform(streams_of[1], (NX, L), jnp.float32) ** block_scale(streams_of[1], (NX, L), ((0, 24),), -0.2, 0.2)), 0.5, 8.0)
    cooling = jnp.clip(jnp.exp(math.log(0.5) - 2.3025851 * jax.random.uniform(streams_of[2], (NX, L), jnp.float32) ** block_scale(streams_of[2], (NX, L), ((0, 24),), -0.2, 0.2)), 0.05, 0.5)
    harm_order = with_ends(jax.random.randint(streams_of[3], (HARMS,), 8, 65), jax.random.fold_in(streams_of[3], 1), 8, 64).astype(jnp.int32)
    harm_amp = with_ends(jax.random.randint(streams_of[4], (HARMS,), 1, 5), jax.random.fold_in(streams_of[4], 1), 1, 4).astype(jnp.int32)
    block_counts = draw_block_counts(jax.random.fold_in(streams_of[6], 71), 0)
    return {"current_pattern": current_pattern, "conductivity": conductivity, "cooling": cooling, "harm_order": harm_order, "harm_amp": harm_amp, "block_counts": block_counts}


base_freq = 0.1


def neighbour_total(field):
    bordered_array = jnp.pad(field, 1)
    return bordered_array[2:, 1:-1] + bordered_array[:-2, 1:-1] + bordered_array[1:-1, 2:] + bordered_array[1:-1, :-2]


def harmonic_loss(current_pattern, conductivity, order, amp, count):
    omega = base_freq * order.astype(jnp.float32)
    columns = jnp.arange(L).astype(jnp.int32)
    mask = (columns < count * BLK).astype(jnp.float32)[None, :]
    source = amp.astype(jnp.float32) * current_pattern * mask
    product = omega * conductivity
    denom = 16.0 + product * product
    inv_re = 4.0 / denom
    inv_im = -product / denom
    real_part = source * inv_re
    imag_part = source * inv_im
    for sweep in range(EDDY_SWEEPS - 1):
        near_re = source + neighbour_total(real_part)
        near_im = neighbour_total(imag_part)
        real_part = mask * (near_re * inv_re - near_im * inv_im)
        imag_part = mask * (near_re * inv_im + near_im * inv_re)
    return 0.5 * omega * omega * conductivity * (real_part * real_part + imag_part * imag_part)


def reference(current_pattern, conductivity, cooling, harm_order, harm_amp, block_counts):
    def accumulate(index, total):
        return total + harmonic_loss(current_pattern, conductivity, harm_order[index], harm_amp[index], block_counts[index])

    total = lax.fori_loop(0, HARMS, accumulate, jnp.zeros(current_pattern.shape, current_pattern.dtype))
    averaged_dissipation = total / HARMS
    inverted_weight = 1.0 / (4.0 + cooling)
    thermal_increase = averaged_dissipation * inverted_weight
    for sweep in range(HEAT_SWEEPS - 1):
        thermal_increase = (averaged_dissipation + neighbour_total(thermal_increase)) * inverted_weight
    return averaged_dissipation, thermal_increase
```

```python
import functools

import jax
import jax.numpy as jnp
from jax import lax
from jax.experimental import pallas as pl
from jax.experimental.pallas import tpu as pltpu
from jax.sharding import PartitionSpec as P

MESH = pl.DeviceIdType.MESH
BASE_FREQ = 0.1
HARMS = 32
SLABS = 24
ROWS = 32
BLK = 128
WIDE = 2 * BLK
PAD = 8
TALL = ROWS + 2 * PAD
NEAR = (0, 1, 7, 2, 6, 3, 5, 4)
FAR = (4, 5, 3, 6, 2, 7, 1, 0)


def place():
    m, h = lax.axis_index("mesh"), lax.axis_index("harm")
    return m, m // 6, ((h // 2) % 2) * 6 + m % 6, h // 4, h % 2


def device(x, z, y, c):
    return (x % 4) * 6 + z % 6, (y % 8) * 4 + (z // 6) * 2 + c % 2


def slot_of(dz, dy, dc):
    return dz * 16 + NEAR.index(dy) * 2 + dc


def kernel(
    current, conductivity, cooling, msg, mean_out, heat_out,
    field, sides, par, cur_b, con_b, inv_r, inv_i, a_r, a_i, b_r, b_i, weight, total, packed, rec, heat,
    load_sem, int_sem, send_sem, recv_sem, edge_send, edge_recv, all_send, all_recv, out_sem,
):
    m, x, z, y, c = place()
    h = lax.axis_index("harm")
    z_lo = z % 6
    low, high = z < 6, z >= 6
    first, last = z_lo == 0, z_lo == 5
    above = ((m + SLABS - 1) % SLABS, h)
    below = ((m + 1) % SLABS, h)
    barrier = pltpu.get_barrier_semaphore()

    loads = []
    own_row = pltpu.make_async_copy(msg, par.at[pl.ds(0, 1)], int_sem)
    left = jnp.maximum(h - 1, 0)
    right = jnp.minimum(h + 1, HARMS - 1)
    for i, source in enumerate((current, conductivity, cooling)):
        for j, (block, target) in enumerate(
            (
                (h, field.at[i, pl.ds(PAD, ROWS), pl.ds(0, BLK)]),
                (left, sides.at[i, 0]),
                (right, sides.at[i, 1]),
            )
        ):
            columns = pl.ds(pl.multiple_of(block * BLK, BLK), BLK)
            loads.append(pltpu.make_async_copy(source.at[:, columns], target, load_sem.at[i, j]))
    for load in loads:
        load.start()

    def greet(who):
        pl.semaphore_signal(barrier, inc=1, device_id=who, device_id_type=MESH)

    around = [(dy, dc) for dy in FAR for dc in (1, 0)]

    @pl.when(low)
    def _():
        for dy, dc in around:
            if dy or dc:
                greet(device(x, z, y + dy, c + dc))
        for dy, dc in around:
            greet(device(x, 11 - z, y + dy, c + dc))

    @pl.when(jnp.logical_not(last))
    def _():
        greet(below)

    @pl.when(first)
    def _():
        greet(above)

    links = jnp.where(first, 0, 1) + jnp.where(last, 1, 0)
    pl.semaphore_wait(barrier, links + jnp.where(low, 15, 16))

    def row_copy(index, dz, dy, dc):
        slot = slot_of(dz, dy, dc)
        to = device(x, 11 - z if dz else z, y + 8 - dy, c + dc)
        return pltpu.make_async_remote_copy(
            msg, par.at[pl.ds(slot, 1)], send_sem.at[index], recv_sem.at[slot], to, MESH
        )

    @pl.when(high)
    def _():
        for index, (dy, dc) in enumerate(around):
            row_copy(index, 1, dy, dc).start()

    @pl.when(low)
    def _():
        own_row.start()
        for index, (dy, dc) in enumerate(around):
            if dy or dc:
                row_copy(index, 0, dy, dc).start()

    for load in loads:
        load.wait()
    half = lax.broadcasted_iota(jnp.int32, (ROWS, BLK), 1) < BLK // 2
    for i in range(3):
        field[i, PAD : PAD + ROWS, BLK:WIDE] = jnp.where(half, sides[i, 1], sides[i, 0])

    to_below = pltpu.make_async_remote_copy(
        field.at[:, pl.ds(ROWS, PAD)], field.at[:, pl.ds(0, PAD)], edge_send.at[0], edge_recv.at[0], below, MESH
    )
    to_above = pltpu.make_async_remote_copy(
        field.at[:, pl.ds(PAD, PAD)], field.at[:, pl.ds(PAD + ROWS, PAD)], edge_send.at[1], edge_recv.at[1], above, MESH
    )

    @pl.when(jnp.logical_not(first))
    def _():
        to_above.start()

    @pl.when(last)
    def _():
        to_below.start()
        to_above.wait_recv()
        to_below.wait_recv()

    @pl.when(first)
    def _():
        to_above.wait_recv()
        to_below.start()
        to_below.wait_recv()
        to_above.start()

    @pl.when(jnp.logical_not(jnp.logical_or(first, last)))
    def _():
        to_above.wait_recv()
        to_below.start()
        to_below.wait_recv()

    for r in range(2, TALL - 2):
        cur_b[r] = jnp.broadcast_to(field[0, r : r + 1, :], (8, WIDE))
        con_b[r] = jnp.broadcast_to(field[1, r : r + 1, :], (8, WIDE))

    ext_lane = lax.broadcasted_iota(jnp.int32, (8, WIDE), 1)
    block = jnp.where(ext_lane < BLK, h, jnp.where(ext_lane < BLK + BLK // 2, h + 1, h - 1)).astype(jnp.float32)
    up_ok = jnp.where(m > 0, 1.0, 0.0)
    down_ok = jnp.where(m < SLABS - 1, 1.0, 0.0)
    all_copy = pltpu.make_async_remote_copy(par, par, all_send, all_recv, device(x, 11 - z, y, c), MESH)

    def neighbours(ref, at, size):
        mid = ref[pl.ds(at, size)]
        return (ref[pl.ds(at - 1, size)] + ref[pl.ds(at + 1, size)]) + (
            pltpu.roll(mid, 1, 2) + pltpu.roll(mid, WIDE - 1, 2)
        )

    def group(g, carry):
        def arrived(i):
            pltpu.make_async_remote_copy(
                msg, par.at[pl.ds(g * 8 + i, 1)], send_sem.at[0], recv_sem.at[g * 8 + i], below, MESH
            ).wait_recv()

        @pl.when(low)
        def _():
            pl.when(g > 0)(lambda: arrived(0))
            pl.when(g == 0)(own_row.wait)
            for i in range(1, 8):
                arrived(i)

            @pl.when(g == 3)
            def _():
                all_copy.start()

        @pl.when(jnp.logical_and(high, g == 0))
        def _():
            all_copy.wait_recv()

        numbers = par[pl.ds(pl.multiple_of(g * 8, 8), 8), :]
        om = jnp.broadcast_to(numbers[:, 0:1], (8, WIDE))
        am = jnp.broadcast_to(numbers[:, 1:2], (8, WIDE))
        ct = jnp.broadcast_to(numbers[:, 2:3], (8, WIDE))
        mask = jnp.where(jnp.logical_and(block >= 0.0, block < ct), 1.0, 0.0)
        scale = (0.5 / HARMS) * (om * om) * (am * am) * mask

        def first_sweep(at, size, ok):
            con, cur = con_b[pl.ds(at, size)], cur_b[pl.ds(at, size)]
            product = om[None] * con
            inverse = 1.0 / (16.0 + product * product)
            masked = inverse * (mask * ok)[None]
            re = 4.0 * masked
            im = -(product * masked)
            inv_r[pl.ds(at, size)] = re
            inv_i[pl.ds(at, size)] = im
            a_r[pl.ds(at, size)] = cur * re
            a_i[pl.ds(at, size)] = cur * im
            weight[pl.ds(at, size)] = (scale[None] * con) * inverse

        first_sweep(2, 3, up_ok)
        first_sweep(5, 3, up_ok)
        lax.fori_loop(0, 8, lambda i, t: (first_sweep(PAD + 4 * i, 4, 1.0), t)[1], 0)
        first_sweep(PAD + ROWS, 3, down_ok)
        first_sweep(PAD + ROWS + 3, 3, down_ok)

        def second_sweep(i, t):
            at, size = 3 + 3 * i, 3
            near_r = cur_b[pl.ds(at, size)] + neighbours(a_r, at, size)
            near_i = neighbours(a_i, at, size)
            re, im = inv_r[pl.ds(at, size)], inv_i[pl.ds(at, size)]
            b_r[pl.ds(at, size)] = near_r * re - near_i * im
            b_i[pl.ds(at, size)] = near_r * im + near_i * re
            return t

        lax.fori_loop(0, 14, second_sweep, 0)

        def third_sweep(i, t):
            at, size = 4 + 4 * i, 4
            near_r = cur_b[pl.ds(at, size)] + neighbours(b_r, at, size)
            near_i = neighbours(b_i, at, size)
            loss = weight[pl.ds(at, size)] * (near_r * near_r + near_i * near_i)
            total[pl.ds(at, size)] = jnp.where(g == 0, loss, total[pl.ds(at, size)] + loss)
            return t

        lax.fori_loop(0, 10, third_sweep, 0)
        return carry

    def start_total(i, t):
        total[pl.ds(4 + 4 * i, 4)] = jnp.zeros((4, 8, WIDE), jnp.float32)
        return t

    lax.fori_loop(0, 10, start_total, 0)
    lax.fori_loop(0, 4, group, 0)

    packed[...] = jnp.zeros_like(packed)
    for r in range(5, TALL - 5):
        packed[r : r + 1, :] = jnp.sum(total[r], axis=0, keepdims=True)
    row = lax.broadcasted_iota(jnp.int32, (TALL, WIDE), 0)
    col = lax.broadcasted_iota(jnp.int32, (TALL, WIDE), 1)
    inside = jnp.logical_and(
        jnp.logical_and(jnp.logical_or(row >= PAD, m > 0), jnp.logical_or(row < PAD + ROWS, m < SLABS - 1)),
        jnp.logical_and(
            jnp.logical_or(col < BLK + BLK // 2, h > 0),
            jnp.logical_or(jnp.logical_or(col < BLK, col >= BLK + BLK // 2), h < HARMS - 1),
        ),
    )
    share = jnp.where(inside, 1.0 / (4.0 + field[2]), 0.0)
    mean = packed[...]
    warm = mean * share
    for sweep in range(3):
        warm = (
            mean
            + (pltpu.roll(warm, 1, 0) + pltpu.roll(warm, TALL - 1, 0))
            + (pltpu.roll(warm, 1, 1) + pltpu.roll(warm, WIDE - 1, 1))
        ) * share
    heat[...] = warm
    results = [
        pltpu.make_async_copy(source.at[pl.ds(PAD, ROWS), pl.ds(0, BLK)], target, out_sem.at[i])
        for i, (source, target) in enumerate(((packed, mean_out), (heat, heat_out)))
    ]
    for result in results:
        result.start()

    for result in results:
        result.wait()
    to_below.wait_send()
    to_above.wait_send()

    @pl.when(high)
    def _():
        for index, (dy, dc) in enumerate(around):
            row_copy(index, 1, dy, dc).wait_send()

    @pl.when(low)
    def _():
        all_copy.wait_send()
        for index, (dy, dc) in enumerate(around):
            if dy or dc:
                row_copy(index, 0, dy, dc).wait_send()


def on_device(current_pattern, conductivity, cooling, harm_order, harm_amp, block_counts):
    f32 = jnp.float32
    lane = lax.broadcasted_iota(jnp.int32, (1, BLK), 1)
    numbers = (BASE_FREQ * harm_order.astype(f32), harm_amp.astype(f32), block_counts.astype(f32))
    row = jnp.where(lane == 0, numbers[0], jnp.where(lane == 1, numbers[1], numbers[2]))
    tall = pltpu.VMEM((TALL, 8, WIDE), f32)
    return pl.pallas_call(
        kernel,
        out_shape=[jax.ShapeDtypeStruct((ROWS, BLK), f32)] * 2,
        in_specs=[pl.BlockSpec(memory_space=pltpu.HBM)] * 4,
        out_specs=[pl.BlockSpec(memory_space=pltpu.HBM)] * 2,
        scratch_shapes=[
            pltpu.VMEM((3, TALL, WIDE), f32),
            pltpu.VMEM((3, 2, ROWS, BLK), f32),
            pltpu.VMEM((HARMS, BLK), f32),
            tall, tall, tall, tall, tall, tall, tall, tall, tall, tall,
            pltpu.VMEM((TALL, WIDE), f32),
            pltpu.VMEM((TALL, WIDE), f32),
            pltpu.VMEM((TALL, WIDE), f32),
            pltpu.SemaphoreType.DMA((3, 3)),
            pltpu.SemaphoreType.DMA,
            pltpu.SemaphoreType.DMA((16,)),
            pltpu.SemaphoreType.DMA((HARMS,)),
            pltpu.SemaphoreType.DMA((2,)),
            pltpu.SemaphoreType.DMA((2,)),
            pltpu.SemaphoreType.DMA,
            pltpu.SemaphoreType.DMA,
            pltpu.SemaphoreType.DMA((2,)),
        ],
        compiler_params=pltpu.CompilerParams(collective_id=0, has_side_effects=True),
    )(current_pattern, conductivity, cooling, row)


def solution(mesh):
    return jax.shard_map(
        on_device,
        mesh=mesh,
        in_specs=(
            P("mesh", None),
            P("mesh", None),
            P("mesh", None),
            P("harm"),
            P("harm"),
            P("harm"),
        ),
        out_specs=(P("mesh", "harm"), P("mesh", "harm")),
        check_vma=False,
    )
```

```python
import functools

import jax
import jax.numpy as jnp
from jax import lax
from jax.experimental import pallas as pl
from jax.experimental.pallas import tpu as pltpu
from jax.sharding import PartitionSpec as P

MESH = pl.DeviceIdType.MESH
BASE_FREQ = 0.1
HARMS = 32
SLABS = 24
ROWS = 32
BLK = 128
WIDE = 2 * BLK
PAD = 8
TALL = ROWS + 2 * PAD
RING = HARMS // 2


def place():
    m, h = lax.axis_index("mesh"), lax.axis_index("harm")
    return m, m // 6, ((h // 2) % 2) * 6 + m % 6, h // 4, h % 2


def device(x, z, y, c):
    return (x % 4) * 6 + z % 6, (y % 8) * 4 + (z // 6) * 2 + c % 2


def offset(i):
    k = i // 2
    return (4 + (k % 2) * ((k + 1) // 2) - (1 - k % 2) * (k // 2)) % 8, 1 - i % 2


def kernel(
    current, conductivity, cooling, order, amp, count, both,
    field, sides, other, other_parts, ints, msg, par, cur_b, con_b, inv_r, inv_i, a_r, a_i, b_r, b_i, weight, total, packed,
    load_sem, other_sem, int_sem, send_sem, recv_sem, edge_send, edge_recv, all_send, all_recv,
):
    m, x, z, y, c = place()
    h = lax.axis_index("harm")
    z_lo = z % 6
    low, high = z < 6, z >= 6
    first, last = z_lo == 0, z_lo == 5
    above = ((m + SLABS - 1) % SLABS, h)
    below = ((m + 1) % SLABS, h)
    barrier = pltpu.get_barrier_semaphore()

    loads = []
    for i, (source, target) in enumerate(zip((order, amp, count), ints)):
        loads.append(pltpu.make_async_copy(source, target, int_sem.at[i]))
    left = jnp.maximum(h - 1, 0)
    right = jnp.minimum(h + 1, HARMS - 1)
    for i, source in enumerate((current, conductivity, cooling)):
        for j, (block, target) in enumerate(
            (
                (h, field.at[i, pl.ds(PAD, ROWS), pl.ds(0, BLK)]),
                (left, sides.at[i, 0]),
                (right, sides.at[i, 1]),
            )
        ):
            columns = pl.ds(pl.multiple_of(block * BLK, BLK), BLK)
            loads.append(pltpu.make_async_copy(source.at[:, columns], target, load_sem.at[i, j]))
    for load in loads:
        load.start()
    lends = jnp.logical_or(z == 6, z == 11)
    lent_rows = pl.ds(pl.multiple_of(jnp.where(z == 6, 0, ROWS - PAD), PAD), PAD)
    other_loads = []
    for i, source in enumerate((current, conductivity, cooling)):
        for j, block in enumerate((h - 2, jnp.maximum(h - 3, 0), h - 1)):
            columns = pl.ds(pl.multiple_of(block * BLK, BLK), BLK)
            other_loads.append(
                pltpu.make_async_copy(source.at[lent_rows, columns], other_parts.at[i, j], other_sem.at[i, j])
            )

    @pl.when(lends)
    def _():
        for load in other_loads:
            load.start()


    def greet(who):
        pl.semaphore_signal(barrier, inc=1, device_id=who, device_id_type=MESH)

    def for_each(count, do):
        def step(i, t):
            do(i)
            return t

        lax.fori_loop(0, count, step, 0)

    @pl.when(jnp.logical_not(last))
    def _():
        greet(below)

    @pl.when(z == 5)
    def _():
        greet(device(x + 1, 6, y, c))

    @pl.when(z == 6)
    def _():
        greet(above)

    @pl.when(z == 0)
    def _():
        greet(device(x + 3, 11, y, c))

    def greet_offset(i, height):
        dy, dc = offset(i)
        greet(device(x, height, y + dy, c + dc))

    @pl.when(low)
    def _():
        for_each(RING - 1, lambda i: greet_offset(i, z))
        for_each(RING, lambda i: greet_offset(i, 11 - z))

    for load in loads[:3]:
        load.wait()
    lane = lax.broadcasted_iota(jnp.int32, (1, BLK), 1)
    omega = BASE_FREQ * jnp.full((1, BLK), ints[0][0], jnp.int32).astype(jnp.float32)
    amps = jnp.full((1, BLK), ints[1][0], jnp.int32).astype(jnp.float32)
    counts = jnp.full((1, BLK), ints[2][0], jnp.int32).astype(jnp.float32)
    msg[...] = jnp.where(lane == 0, omega, jnp.where(lane == 1, amps, counts))

    links = jnp.where(z == 0, 0, 1) + jnp.where(z == 11, 2, 0)
    pl.semaphore_wait(barrier, links + jnp.where(low, 15, 16))

    def row_copy(i, other_half):
        dy, dc = offset(i)
        slot = RING * other_half + RING - 1 - i
        to = device(x, 11 - z if other_half else z, y + 8 - dy, c + dc)
        return pltpu.make_async_remote_copy(
            msg, par.at[pl.ds(slot, 1)], send_sem.at[RING * other_half + i], recv_sem.at[slot], to, MESH
        )

    @pl.when(high)
    def _():
        for_each(RING, lambda i: row_copy(i, 1).start())

    @pl.when(low)
    def _():
        par[0:1, :] = msg[...]
        for_each(RING - 1, lambda i: row_copy(i, 0).start())

    for load in loads[3:]:
        load.wait()
    half = lax.broadcasted_iota(jnp.int32, (ROWS, BLK), 1) < BLK // 2
    for i in range(3):
        field[i, PAD : PAD + ROWS, BLK:WIDE] = jnp.where(half, sides[i, 1], sides[i, 0])

    to_below = pltpu.make_async_remote_copy(
        field.at[:, pl.ds(ROWS, PAD)], field.at[:, pl.ds(0, PAD)], edge_send.at[0], edge_recv.at[0], below, MESH
    )
    to_above = pltpu.make_async_remote_copy(
        field.at[:, pl.ds(PAD, PAD)], field.at[:, pl.ds(PAD + ROWS, PAD)], edge_send.at[1], edge_recv.at[1], above, MESH
    )

    to_fifth = pltpu.make_async_remote_copy(
        other,
        field.at[:, pl.ds(PAD + ROWS, PAD)],
        edge_send.at[2],
        edge_recv.at[1],
        device(x + 3, 5, y, c),
        MESH,
    )

    to_zero = pltpu.make_async_remote_copy(
        other, field.at[:, pl.ds(0, PAD)], edge_send.at[2], edge_recv.at[0], device(x + 1, 0, y, c), MESH
    )

    @pl.when(jnp.logical_not(first))
    def _():
        to_above.start()

    @pl.when(lends)
    def _():
        for load in other_loads:
            load.wait()
        for i in range(3):
            other[i, :, 0:BLK] = other_parts[i, 0]
            other[i, :, BLK:WIDE] = jnp.where(half[0:PAD], other_parts[i, 2], other_parts[i, 1])
        pl.when(z == 6)(to_fifth.start)
        pl.when(z == 11)(to_zero.start)

    @pl.when(z == 11)
    def _():
        to_below.start()

    to_above.wait_recv()

    @pl.when(jnp.logical_not(last))
    def _():
        to_below.start()

    to_below.wait_recv()

    @pl.when(z == 6)
    def _():
        to_above.start()

    for r in range(2, TALL - 2):
        cur_b[r] = jnp.broadcast_to(field[0, r : r + 1, :], (8, WIDE))
        con_b[r] = jnp.broadcast_to(field[1, r : r + 1, :], (8, WIDE))

    ext_lane = lax.broadcasted_iota(jnp.int32, (8, WIDE), 1)
    block = jnp.where(ext_lane < BLK, h, jnp.where(ext_lane < BLK + BLK // 2, h + 1, h - 1)).astype(jnp.float32)
    up_ok = jnp.where(m > 0, 1.0, 0.0)
    down_ok = jnp.where(m < SLABS - 1, 1.0, 0.0)
    all_copy = pltpu.make_async_remote_copy(
        par, par, all_send, all_recv, device(x, 11 - z, y, c), MESH
    )

    def neighbours(ref, at, size):
        mid = ref[pl.ds(at, size)]
        return (ref[pl.ds(at - 1, size)] + ref[pl.ds(at + 1, size)]) + (
            pltpu.roll(mid, 1, 2) + pltpu.roll(mid, WIDE - 1, 2)
        )

    def group(g, carry):
        def arrived(i):
            pltpu.make_async_remote_copy(
                msg, par.at[pl.ds(g * 8 + i, 1)], send_sem.at[0], recv_sem.at[g * 8 + i], below, MESH
            ).wait_recv()

        @pl.when(low)
        def _():
            pl.when(g > 0)(lambda: arrived(0))
            for_each(7, lambda i: arrived(i + 1))

        @pl.when(jnp.logical_and(low, g == 3))
        def _():
            all_copy.start()

        @pl.when(jnp.logical_and(high, g == 0))
        def _():
            all_copy.wait_recv()

        numbers = par[pl.ds(pl.multiple_of(g * 8, 8), 8), :]
        om = jnp.broadcast_to(numbers[:, 0:1], (8, WIDE))
        am = jnp.broadcast_to(numbers[:, 1:2], (8, WIDE))
        ct = jnp.broadcast_to(numbers[:, 2:3], (8, WIDE))
        mask = jnp.where(jnp.logical_and(block >= 0.0, block < ct), 1.0, 0.0)
        scale = 0.5 * (om * om) * (am * am) * mask

        def first_sweep(at, size, ok):
            con, cur = con_b[pl.ds(at, size)], cur_b[pl.ds(at, size)]
            product = om[None] * con
            inverse = 1.0 / (16.0 + product * product)
            masked = inverse * (mask * ok)[None]
            re = 4.0 * masked
            im = -(product * masked)
            inv_r[pl.ds(at, size)] = re
            inv_i[pl.ds(at, size)] = im
            a_r[pl.ds(at, size)] = cur * re
            a_i[pl.ds(at, size)] = cur * im
            weight[pl.ds(at, size)] = (scale[None] * con) * inverse

        first_sweep(2, 3, up_ok)
        first_sweep(5, 3, up_ok)
        lax.fori_loop(0, 8, lambda i, t: (first_sweep(PAD + 4 * i, 4, 1.0), t)[1], 0, unroll=True)
        first_sweep(PAD + ROWS, 3, down_ok)
        first_sweep(PAD + ROWS + 3, 3, down_ok)

        def second_sweep(i, t):
            at, size = 3 + 3 * i, 3
            near_r = cur_b[pl.ds(at, size)] + neighbours(a_r, at, size)
            near_i = neighbours(a_i, at, size)
            re, im = inv_r[pl.ds(at, size)], inv_i[pl.ds(at, size)]
            b_r[pl.ds(at, size)] = near_r * re - near_i * im
            b_i[pl.ds(at, size)] = near_r * im + near_i * re
            return t

        lax.fori_loop(0, 14, second_sweep, 0, unroll=True)

        def third_sweep(i, t):
            at, size = 4 + 4 * i, 4
            near_r = cur_b[pl.ds(at, size)] + neighbours(b_r, at, size)
            near_i = neighbours(b_i, at, size)
            loss = weight[pl.ds(at, size)] * (near_r * near_r + near_i * near_i)
            total[pl.ds(at, size)] = jnp.where(g == 0, loss, total[pl.ds(at, size)] + loss)
            return t

        lax.fori_loop(0, 10, third_sweep, 0, unroll=True)
        return carry

    def start_total(i, t):
        total[pl.ds(4 + 4 * i, 4)] = jnp.zeros((4, 8, WIDE), jnp.float32)
        return t

    lax.fori_loop(0, 10, start_total, 0)
    lax.fori_loop(0, 4, group, 0)

    packed[...] = jnp.zeros_like(packed)
    for r in range(5, TALL - 5):
        packed[r : r + 1, :] = jnp.sum(total[r], axis=0, keepdims=True)
    row = lax.broadcasted_iota(jnp.int32, (TALL, WIDE), 0)
    col = lax.broadcasted_iota(jnp.int32, (TALL, WIDE), 1)
    inside = jnp.logical_and(
        jnp.logical_and(jnp.logical_or(row >= PAD, m > 0), jnp.logical_or(row < PAD + ROWS, m < SLABS - 1)),
        jnp.logical_and(
            jnp.logical_or(col < BLK + BLK // 2, h > 0),
            jnp.logical_or(jnp.logical_or(col < BLK, col >= BLK + BLK // 2), h < HARMS - 1),
        ),
    )
    share = jnp.where(inside, 1.0 / (4.0 + field[2]), 0.0)
    mean = packed[...]
    warm = mean * share
    for sweep in range(3):
        warm = (
            mean
            + (pltpu.roll(warm, 1, 0) + pltpu.roll(warm, TALL - 1, 0))
            + (pltpu.roll(warm, 1, 1) + pltpu.roll(warm, WIDE - 1, 1))
        ) * share
    both[0] = mean[PAD : PAD + ROWS, 0:BLK]
    both[1] = warm[PAD : PAD + ROWS, 0:BLK]

    @pl.when(z != 5)
    def _():
        to_below.wait_send()

    @pl.when(z == 11)
    def _():
        to_zero.wait_send()


    @pl.when(z != 0)
    def _():
        to_above.wait_send()

    @pl.when(z == 6)
    def _():
        to_fifth.wait_send()

    @pl.when(high)
    def _():
        for_each(RING, lambda i: row_copy(i, 1).wait_send())

    @pl.when(low)
    def _():
        all_copy.wait_send()
        for_each(RING - 1, lambda i: row_copy(i, 0).wait_send())


def exchange_and_solve(current_pattern, conductivity, cooling, harm_order, harm_amp, block_counts):
    f32 = jnp.float32
    tall = pltpu.VMEM((TALL, 8, WIDE), f32)
    return pl.pallas_call(
        kernel,
        out_shape=jax.ShapeDtypeStruct((2, ROWS, BLK), f32),
        in_specs=[pl.BlockSpec(memory_space=pltpu.HBM)] * 6,
        out_specs=pl.BlockSpec(memory_space=pltpu.VMEM),
        scratch_shapes=[
            pltpu.VMEM((3, TALL, WIDE), f32),
            pltpu.VMEM((3, 2, ROWS, BLK), f32),
            pltpu.VMEM((3, PAD, WIDE), f32),
            pltpu.VMEM((3, 3, PAD, BLK), f32),
            [pltpu.SMEM((1,), jnp.int32)] * 3,
            pltpu.VMEM((1, BLK), f32),
            pltpu.VMEM((HARMS, BLK), f32),
            tall, tall, tall, tall, tall, tall, tall, tall, tall, tall,
            pltpu.VMEM((TALL, WIDE), f32),
            pltpu.SemaphoreType.DMA((3, 3)),
            pltpu.SemaphoreType.DMA((3, 3)),
            pltpu.SemaphoreType.DMA((3,)),
            pltpu.SemaphoreType.DMA((HARMS,)),
            pltpu.SemaphoreType.DMA((HARMS,)),
            pltpu.SemaphoreType.DMA((3,)),
            pltpu.SemaphoreType.DMA((2,)),
            pltpu.SemaphoreType.DMA,
            pltpu.SemaphoreType.DMA,
        ],
        compiler_params=pltpu.CompilerParams(collective_id=0, has_side_effects=True),
    )(current_pattern, conductivity, cooling, harm_order, harm_amp, block_counts)


def on_device(*args):
    both = lax.cond(
        lax.axis_index("harm") < HARMS,
        exchange_and_solve,
        lambda *a: jnp.zeros((2, ROWS, BLK), jnp.float32),
        *args,
    )
    return both[0] * (1.0 / HARMS), both[1] * (1.0 / HARMS)


def solution(mesh):
    return jax.shard_map(
        on_device,
        mesh=mesh,
        in_specs=(
            P("mesh", None),
            P("mesh", None),
            P("mesh", None),
            P("harm"),
            P("harm"),
            P("harm"),
        ),
        out_specs=(P("mesh", "harm"), P("mesh", "harm")),
        check_vma=False,
    )
```

```python
import functools

import jax
import jax.numpy as jnp
from jax import lax
from jax.experimental import pallas as pl
from jax.experimental.pallas import tpu as pltpu
from jax.sharding import PartitionSpec as P

MESH = pl.DeviceIdType.MESH
BASE_FREQ = 0.1
HARMS = 32
SLABS = 24
ROWS = 32
BLK = 128
WIDE = 2 * BLK
PAD = 8
TALL = ROWS + 2 * PAD
RING = HARMS // 2


AROUND = tuple((dy, dc) for dy in (4, 5, 3, 6, 2, 7, 1, 0) for dc in (1, 0))


def steps_below(value, step, count):
    return sum((value >= step * k).astype(jnp.int32) for k in range(1, count))


def kernel(
    current, conductivity, cooling, order, amp, count, both,
    field, parts, other, other_parts, msg, par, cur_b, con_b, inv_r, inv_i, a_r, a_i, b_r, b_i, weight, total, packed,
    load_sem, other_sem, send_sem, recv_sem, edge_send, edge_recv, all_send, all_recv,
):
    m, h = lax.axis_index("mesh"), lax.axis_index("harm")
    x, y = steps_below(m, 6, 4), steps_below(h, 4, 8)
    z_lo = m - 6 * x
    z_hi = (h - 4 * y >= 2).astype(jnp.int32)
    c = h - 4 * y - 2 * z_hi
    z = z_lo + 6 * z_hi
    low, high = z < 6, z >= 6
    last = z_lo == 5
    above = (jnp.where(m == 0, SLABS - 1, m - 1), h)
    below = (jnp.where(m == SLABS - 1, 0, m + 1), h)
    after = jnp.where(x == 3, m - 18, m + 6) - 5
    before = jnp.where(x == 0, m + 18, m - 6) + 5
    own_half = [2 * z_hi + c, 2 * z_hi + (1 - c)]
    other_half = [2 * (1 - z_hi) + c, 2 * (1 - z_hi) + (1 - c)]
    around_y = [4 * jnp.where(y + d >= 8, y + d - 8, y + d) for d in range(8)]
    mirror = jnp.where(z_lo < 3, m + 3, m - 3)

    def inside(dy, dc):
        return m, around_y[dy % 8] + own_half[dc]

    def across(dy, dc):
        return mirror, around_y[dy % 8] + other_half[dc]

    barrier = pltpu.get_barrier_semaphore()

    left = jnp.maximum(h - 1, 0)
    right = jnp.minimum(h + 1, HARMS - 1)
    for i, source in enumerate((current, conductivity, cooling)):
        for j, block in enumerate((h, left, right)):
            columns = pl.ds(pl.multiple_of(block * BLK, BLK), BLK)
            pltpu.make_async_copy(source.at[:, columns], parts.at[i, j], load_sem).start()
    lends = jnp.logical_or(z == 6, z == 11)
    lent_rows = pl.ds(pl.multiple_of(jnp.where(z == 6, 0, ROWS - PAD), PAD), PAD)

    @pl.when(lends)
    def _():
        for i, source in enumerate((current, conductivity, cooling)):
            for j, block in enumerate((h - 2, jnp.maximum(h - 3, 0), h - 1)):
                columns = pl.ds(pl.multiple_of(block * BLK, BLK), BLK)
                pltpu.make_async_copy(source.at[lent_rows, columns], other_parts.at[i, j], other_sem).start()

    def greet(who):
        pl.semaphore_signal(barrier, inc=1, device_id=who, device_id_type=MESH)

    @pl.when(jnp.logical_not(last))
    def _():
        greet(below)

    @pl.when(z == 5)
    def _():
        greet((after, h + 2))

    @pl.when(z == 6)
    def _():
        greet(above)

    @pl.when(z == 0)
    def _():
        greet((before, h + 2))

    @pl.when(low)
    def _():
        for dy, dc in AROUND[:-1]:
            greet(inside(dy, dc))
        for dy, dc in AROUND:
            greet(across(dy, dc))

    lane = lax.broadcasted_iota(jnp.int32, (1, BLK), 1)
    numbers = [jnp.full((1, BLK), v[0], jnp.int32) for v in (order, amp, count)]
    msg[...] = jnp.where(lane == 0, numbers[0], jnp.where(lane == 1, numbers[1], numbers[2])).astype(jnp.float32)

    links = jnp.where(z == 0, 0, 1) + jnp.where(z == 11, 2, 0)
    pl.semaphore_wait(barrier, links + jnp.where(low, 15, 16))

    def row_copy(i, crossing):
        dy, dc = AROUND[i]
        slot = RING * crossing + RING - 1 - i
        return pltpu.make_async_remote_copy(
            msg,
            par.at[pl.ds(slot, 1)],
            send_sem,
            recv_sem.at[slot // 8],
            (across if crossing else inside)(-dy, dc),
            MESH,
        )

    @pl.when(high)
    def _():
        for i in range(RING):
            row_copy(i, 1).start()

    @pl.when(low)
    def _():
        par[0:1, :] = msg[...]
        for i in range(RING - 1):
            row_copy(i, 0).start()

    pltpu.make_async_copy(parts, parts, load_sem).wait()
    half = lax.broadcasted_iota(jnp.int32, (ROWS, BLK), 1) < BLK // 2
    for i in range(3):
        field[i, PAD : PAD + ROWS, 0:BLK] = parts[i, 0]
        field[i, PAD : PAD + ROWS, BLK:WIDE] = jnp.where(half, parts[i, 2], parts[i, 1])

    to_below = pltpu.make_async_remote_copy(
        field.at[:, pl.ds(ROWS, PAD)], field.at[:, pl.ds(0, PAD)], edge_send.at[0], edge_recv.at[0], below, MESH
    )
    to_above = pltpu.make_async_remote_copy(
        field.at[:, pl.ds(PAD, PAD)], field.at[:, pl.ds(PAD + ROWS, PAD)], edge_send.at[1], edge_recv.at[1], above, MESH
    )

    to_fifth = pltpu.make_async_remote_copy(
        other,
        field.at[:, pl.ds(PAD + ROWS, PAD)],
        edge_send.at[2],
        edge_recv.at[1],
        (before, h - 2),
        MESH,
    )

    to_zero = pltpu.make_async_remote_copy(
        other, field.at[:, pl.ds(0, PAD)], edge_send.at[2], edge_recv.at[0], (after, h - 2), MESH
    )

    @pl.when(z_lo != 0)
    def _():
        to_above.start()

    @pl.when(lends)
    def _():
        pltpu.make_async_copy(other_parts, other_parts, other_sem).wait()
        for i in range(3):
            other[i, :, 0:BLK] = other_parts[i, 0]
            other[i, :, BLK:WIDE] = jnp.where(half[0:PAD], other_parts[i, 2], other_parts[i, 1])
        pl.when(z == 6)(to_fifth.start)
        pl.when(z == 11)(to_zero.start)

    @pl.when(z == 11)
    def _():
        to_below.start()

    to_above.wait_recv()

    @pl.when(jnp.logical_not(last))
    def _():
        to_below.start()

    ext_lane = lax.broadcasted_iota(jnp.int32, (8, WIDE), 1)
    block = jnp.where(ext_lane < BLK, h, jnp.where(ext_lane < BLK + BLK // 2, h + 1, h - 1)).astype(jnp.float32)
    up_ok = jnp.where(m > 0, 1.0, 0.0)
    down_ok = jnp.where(m < SLABS - 1, 1.0, 0.0)
    all_copy = pltpu.make_async_remote_copy(
        par, par, all_send, all_recv, across(0, 0), MESH
    )

    def neighbours(ref, at, size):
        mid = ref[pl.ds(at, size)]
        return (ref[pl.ds(at - 1, size)] + ref[pl.ds(at + 1, size)]) + (
            pltpu.roll(mid, 1, 2) + pltpu.roll(mid, WIDE - 1, 2)
        )

    def lift(rows):
        for r in rows:
            cur_b[r] = jnp.broadcast_to(field[0, r : r + 1, :], (8, WIDE))
            con_b[r] = jnp.broadcast_to(field[1, r : r + 1, :], (8, WIDE))

    def sweeps(g, spans_a, spans_b, spans_q):
        numbers = par[pl.ds(pl.multiple_of(g * 8, 8), 8), :]
        om = jnp.broadcast_to(BASE_FREQ * numbers[:, 0:1], (8, WIDE))
        am = jnp.broadcast_to(numbers[:, 1:2], (8, WIDE))
        ct = jnp.broadcast_to(numbers[:, 2:3], (8, WIDE))
        mask = jnp.where(jnp.logical_and(block >= 0.0, block < ct), 1.0, 0.0)
        scale = 0.5 * (om * om) * (am * am) * mask

        def first_sweep(at, size, ok):
            con, cur = con_b[pl.ds(at, size)], cur_b[pl.ds(at, size)]
            product = om[None] * con
            inverse = 1.0 / (16.0 + product * product)
            masked = inverse * (mask * ok)[None]
            re = 4.0 * masked
            im = -(product * masked)
            inv_r[pl.ds(at, size)] = re
            inv_i[pl.ds(at, size)] = im
            a_r[pl.ds(at, size)] = cur * re
            a_i[pl.ds(at, size)] = cur * im
            weight[pl.ds(at, size)] = (scale[None] * con) * inverse

        def second_sweep(at, size):
            near_r = cur_b[pl.ds(at, size)] + neighbours(a_r, at, size)
            near_i = neighbours(a_i, at, size)
            re, im = inv_r[pl.ds(at, size)], inv_i[pl.ds(at, size)]
            b_r[pl.ds(at, size)] = near_r * re - near_i * im
            b_i[pl.ds(at, size)] = near_r * im + near_i * re

        def third_sweep(at, size):
            near_r = cur_b[pl.ds(at, size)] + neighbours(b_r, at, size)
            near_i = neighbours(b_i, at, size)
            loss = weight[pl.ds(at, size)] * (near_r * near_r + near_i * near_i)
            total[pl.ds(at, size)] = total[pl.ds(at, size)] + loss

        for span in spans_a:
            first_sweep(*span)
        for span in spans_b:
            second_sweep(*span)
        for span in spans_q:
            third_sweep(*span)

    end = PAD + ROWS

    def middle(g):
        sweeps(
            g,
            [(at, 4, 1.0) for at in range(PAD, end, 4)],
            [(at, 3) for at in range(PAD + 1, end - 1, 3)],
            [(at, 4) for at in range(PAD + 2, end - 2, 4)],
        )

    def rims(g):
        sweeps(
            g,
            [(3, 3, up_ok), (6, 2, up_ok), (8, 4, 1.0), (end - 4, 4, 1.0), (end, 2, down_ok), (end + 2, 3, down_ok)],
            [(4, 4), (8, 3), (end - 3, 4), (end + 1, 3)],
            [(5, 5), (end - 2, 5)],
        )

    def rows_of(g):
        def rows_here(at, size):
            rows = par.at[pl.ds(at, size)]
            pltpu.make_async_remote_copy(rows, rows, send_sem, recv_sem.at[g], below, MESH).wait_recv()

        @pl.when(low)
        def _():
            @pl.when(g == 0)
            def _():
                rows_here(1, 7)

            pl.when(g > 0)(lambda: rows_here(0, 8))

        @pl.when(jnp.logical_and(low, g == 3))
        def _():
            all_copy.start()

        @pl.when(jnp.logical_and(high, g == 0))
        def _():
            all_copy.wait_recv()


    def early(g, t):
        rows_of(g)
        middle(g)
        return t

    def early_rims(g, t):
        rims(g)
        return t

    def late(g, t):
        rows_of(g)
        middle(g)
        rims(g)
        return t

    def start_total(i, t):
        total[pl.ds(4 + 4 * i, 4)] = jnp.zeros((4, 8, WIDE), jnp.float32)
        return t

    lax.fori_loop(0, 10, start_total, 0)
    lift(range(PAD, end))

    ahead = jnp.where(low, 2, 0)
    lax.fori_loop(0, ahead, early, 0)

    to_below.wait_recv()

    @pl.when(z == 6)
    def _():
        to_above.start()

    lift([*range(3, PAD), *range(end, end + 5)])
    lax.fori_loop(0, ahead, early_rims, 0)
    lax.fori_loop(ahead, 4, late, 0)

    packed[...] = jnp.zeros_like(packed)
    for r in range(5, TALL - 5):
        packed[r : r + 1, :] = jnp.sum(total[r], axis=0, keepdims=True)
    row = lax.broadcasted_iota(jnp.int32, (TALL, WIDE), 0)
    col = lax.broadcasted_iota(jnp.int32, (TALL, WIDE), 1)
    in_grid = jnp.logical_and(
        jnp.logical_and(jnp.logical_or(row >= PAD, m > 0), jnp.logical_or(row < PAD + ROWS, m < SLABS - 1)),
        jnp.logical_and(
            jnp.logical_or(col < BLK + BLK // 2, h > 0),
            jnp.logical_or(jnp.logical_or(col < BLK, col >= BLK + BLK // 2), h < HARMS - 1),
        ),
    )
    share = jnp.where(in_grid, 1.0 / (4.0 + field[2]), 0.0)
    mean = packed[...]
    warm = mean * share
    for sweep in range(3):
        warm = (
            mean
            + (pltpu.roll(warm, 1, 0) + pltpu.roll(warm, TALL - 1, 0))
            + (pltpu.roll(warm, 1, 1) + pltpu.roll(warm, WIDE - 1, 1))
        ) * share
    both[0] = mean[PAD : PAD + ROWS, 0:BLK]
    both[1] = warm[PAD : PAD + ROWS, 0:BLK]

    def rows_sent(size):
        rows = par.at[pl.ds(0, size)]
        pltpu.make_async_remote_copy(rows, rows, send_sem, recv_sem.at[0], below, MESH).wait_send()

    @pl.when(z != 5)
    def _():
        to_below.wait_send()

    @pl.when(z == 11)
    def _():
        to_zero.wait_send()


    @pl.when(z != 0)
    def _():
        to_above.wait_send()

    @pl.when(z == 6)
    def _():
        to_fifth.wait_send()

    @pl.when(high)
    def _():
        rows_sent(RING)

    @pl.when(low)
    def _():
        all_copy.wait_send()
        rows_sent(RING - 1)


def exchange_and_solve(current_pattern, conductivity, cooling, harm_order, harm_amp, block_counts):
    f32 = jnp.float32
    tall = pltpu.VMEM((TALL, 8, WIDE), f32)
    return pl.pallas_call(
        kernel,
        out_shape=jax.ShapeDtypeStruct((2, ROWS, BLK), f32),
        in_specs=[pl.BlockSpec(memory_space=pltpu.HBM)] * 3 + [pl.BlockSpec(memory_space=pltpu.SMEM)] * 3,
        out_specs=pl.BlockSpec(memory_space=pltpu.VMEM),
        scratch_shapes=[
            pltpu.VMEM((3, TALL, WIDE), f32),
            pltpu.VMEM((3, 3, ROWS, BLK), f32),
            pltpu.VMEM((3, PAD, WIDE), f32),
            pltpu.VMEM((3, 3, PAD, BLK), f32),
            pltpu.VMEM((1, BLK), f32),
            pltpu.VMEM((HARMS, BLK), f32),
            tall, tall, tall, tall, tall, tall, tall, tall, tall, tall,
            pltpu.VMEM((TALL, WIDE), f32),
            pltpu.SemaphoreType.DMA,
            pltpu.SemaphoreType.DMA,
            pltpu.SemaphoreType.DMA,
            pltpu.SemaphoreType.DMA((4,)),
            pltpu.SemaphoreType.DMA((3,)),
            pltpu.SemaphoreType.DMA((2,)),
            pltpu.SemaphoreType.DMA,
            pltpu.SemaphoreType.DMA,
        ],
        compiler_params=pltpu.CompilerParams(collective_id=0, has_side_effects=True),
    )(current_pattern, conductivity, cooling, harm_order, harm_amp, block_counts)


def on_device(*args):
    both = lax.cond(
        lax.axis_index("harm") < HARMS,
        exchange_and_solve,
        lambda *a: jnp.zeros((2, ROWS, BLK), jnp.float32),
        *args,
    )
    return both[0] * (1.0 / HARMS), both[1] * (1.0 / HARMS)


def solution(mesh):
    return jax.shard_map(
        on_device,
        mesh=mesh,
        in_specs=(
            P("mesh", None),
            P("mesh", None),
            P("mesh", None),
            P("harm"),
            P("harm"),
            P("harm"),
        ),
        out_specs=(P("mesh", "harm"), P("mesh", "harm")),
        check_vma=False,
    )
```

```python
import functools

import jax
import jax.numpy as jnp
from jax import lax
from jax.experimental import pallas as pl
from jax.experimental.pallas import tpu as pltpu
from jax.sharding import PartitionSpec as P

MESH = pl.DeviceIdType.MESH
BASE_FREQ = 0.1
HARMS = 32
SLABS = 24
ROWS = 32
BLK = 128
WIDE = 2 * BLK
PAD = 8
TALL = ROWS + 2 * PAD
RING = HARMS // 2


AROUND = tuple((dy, dc) for dy in (4, 5, 3, 6, 2, 7, 1, 0) for dc in (1, 0))


def steps_below(value, step, count):
    return sum((value >= step * k).astype(jnp.int32) for k in range(1, count))


def kernel(
    current, conductivity, cooling, order, amp, count, both,
    field, parts, other, other_parts, msg, par, cur_b, con_b, inv_r, inv_i, a_r, a_i, b_r, b_i, weight, total, packed, rec,
    load_sem, other_sem, send_sem, recv_sem, edge_send, edge_recv, all_send, all_recv,
):
    m, h = lax.axis_index("mesh"), lax.axis_index("harm")
    x, y = steps_below(m, 6, 4), steps_below(h, 4, 8)
    z_lo = m - 6 * x
    z_hi = (h - 4 * y >= 2).astype(jnp.int32)
    c = h - 4 * y - 2 * z_hi
    z = z_lo + 6 * z_hi
    low, high = z < 6, z >= 6
    last = z_lo == 5
    above = (jnp.where(m == 0, SLABS - 1, m - 1), h)
    below = (jnp.where(m == SLABS - 1, 0, m + 1), h)
    after = jnp.where(x == 3, m - 18, m + 6) - 5
    before = jnp.where(x == 0, m + 18, m - 6) + 5
    own_half = [2 * z_hi + c, 2 * z_hi + (1 - c)]
    other_half = [2 * (1 - z_hi) + c, 2 * (1 - z_hi) + (1 - c)]
    around_y = [4 * jnp.where(y + d >= 8, y + d - 8, y + d) for d in range(8)]
    low_move = jnp.where(z_lo == 0, 4, jnp.where(z_lo == 1, 2, jnp.where(z_lo == 2, 3, -3)))
    high_move = jnp.where(z_lo == 4, -4, jnp.where(z_lo == 3, -2, jnp.where(z_lo == 5, -3, 3)))
    mirror = m + jnp.where(low, low_move, high_move)

    def inside(dy, dc):
        return m, around_y[dy % 8] + own_half[dc]

    def across(dy, dc):
        return mirror, around_y[dy % 8] + other_half[dc]

    barrier = pltpu.get_barrier_semaphore()

    left = jnp.maximum(h - 1, 0)
    right = jnp.minimum(h + 1, HARMS - 1)
    for i, source in enumerate((current, conductivity, cooling)):
        for j, block in enumerate((h, left, right)):
            columns = pl.ds(pl.multiple_of(block * BLK, BLK), BLK)
            pltpu.make_async_copy(source.at[:, columns], parts.at[i, j], load_sem).start()
    lends = jnp.logical_or(z == 6, z == 11)
    lent_rows = pl.ds(pl.multiple_of(jnp.where(z == 6, 0, ROWS - PAD), PAD), PAD)

    @pl.when(lends)
    def _():
        for i, source in enumerate((current, conductivity, cooling)):
            for j, block in enumerate((h - 2, jnp.maximum(h - 3, 0), h - 1)):
                columns = pl.ds(pl.multiple_of(block * BLK, BLK), BLK)
                pltpu.make_async_copy(source.at[lent_rows, columns], other_parts.at[i, j], other_sem).start()

    def greet(who):
        pl.semaphore_signal(barrier, inc=1, device_id=who, device_id_type=MESH)

    @pl.when(jnp.logical_not(last))
    def _():
        greet(below)

    @pl.when(z == 5)
    def _():
        greet((after, h + 2))

    @pl.when(z == 6)
    def _():
        greet(above)

    @pl.when(z == 0)
    def _():
        greet((before, h + 2))

    @pl.when(low)
    def _():
        for dy, dc in AROUND[:-1]:
            greet(inside(dy, dc))
        for dy, dc in AROUND:
            greet(across(dy, dc))

    lane = lax.broadcasted_iota(jnp.int32, (1, BLK), 1)
    numbers = [jnp.full((1, BLK), v[0], jnp.int32) for v in (order, amp, count)]
    msg[...] = jnp.where(lane == 0, numbers[0], jnp.where(lane == 1, numbers[1], numbers[2])).astype(jnp.float32)

    links = jnp.where(z == 0, 0, 1) + jnp.where(z == 11, 2, 0)
    pl.semaphore_wait(barrier, links + jnp.where(low, 15, 16))

    def row_copy(i, crossing):
        dy, dc = AROUND[i]
        slot = RING * crossing + RING - 1 - i
        return pltpu.make_async_remote_copy(
            msg,
            par.at[pl.ds(slot, 1)],
            send_sem,
            recv_sem.at[slot // 8],
            (across if crossing else inside)(-dy, dc),
            MESH,
        )

    half = lax.broadcasted_iota(jnp.int32, (ROWS, BLK), 1) < BLK // 2
    to_fifth = pltpu.make_async_remote_copy(
        other,
        field.at[:, pl.ds(PAD + ROWS, PAD)],
        edge_send.at[2],
        edge_recv.at[1],
        (before, h - 2),
        MESH,
    )

    to_zero = pltpu.make_async_remote_copy(
        other, field.at[:, pl.ds(0, PAD)], edge_send.at[2], edge_recv.at[0], (after, h - 2), MESH
    )

    @pl.when(lends)
    def _():
        pltpu.make_async_copy(other_parts, other_parts, other_sem).wait()
        for i in range(3):
            other[i, :, 0:BLK] = other_parts[i, 0]
            other[i, :, BLK:WIDE] = jnp.where(half[0:PAD], other_parts[i, 2], other_parts[i, 1])
        pl.when(z == 6)(to_fifth.start)
        pl.when(z == 11)(to_zero.start)

    @pl.when(high)
    def _():
        for i in range(RING):
            row_copy(i, 1).start()

    @pl.when(low)
    def _():
        par[0:1, :] = msg[...]
        for i in range(RING - 1):
            row_copy(i, 0).start()

    pltpu.make_async_copy(parts, parts, load_sem).wait()
    for i in range(3):
        field[i, PAD : PAD + ROWS, 0:BLK] = parts[i, 0]
        field[i, PAD : PAD + ROWS, BLK:WIDE] = jnp.where(half, parts[i, 2], parts[i, 1])

    to_below = pltpu.make_async_remote_copy(
        field.at[:, pl.ds(ROWS, PAD)], field.at[:, pl.ds(0, PAD)], edge_send.at[0], edge_recv.at[0], below, MESH
    )
    to_above = pltpu.make_async_remote_copy(
        field.at[:, pl.ds(PAD, PAD)], field.at[:, pl.ds(PAD + ROWS, PAD)], edge_send.at[1], edge_recv.at[1], above, MESH
    )

    @pl.when(z_lo != 0)
    def _():
        to_above.start()

    @pl.when(z == 11)
    def _():
        to_below.start()

    to_above.wait_recv()

    @pl.when(jnp.logical_not(last))
    def _():
        to_below.start()

    ext_lane = lax.broadcasted_iota(jnp.int32, (8, WIDE), 1)
    block = jnp.where(ext_lane < BLK, h, jnp.where(ext_lane < BLK + BLK // 2, h + 1, h - 1)).astype(jnp.float32)
    up_ok = jnp.where(m > 0, 1.0, 0.0)
    down_ok = jnp.where(m < SLABS - 1, 1.0, 0.0)
    all_copy = pltpu.make_async_remote_copy(
        par, par, all_send, all_recv, across(0, 0), MESH
    )

    def neighbours(ref, at, size):
        mid = ref[pl.ds(at, size)]
        return (ref[pl.ds(at - 1, size)] + ref[pl.ds(at + 1, size)]) + (
            pltpu.roll(mid, 1, 2) + pltpu.roll(mid, WIDE - 1, 2)
        )

    def lift(rows):
        for r in rows:
            cur_b[r] = jnp.broadcast_to(field[0, r : r + 1, :], (8, WIDE))
            con_b[r] = jnp.broadcast_to(field[1, r : r + 1, :], (8, WIDE))

    def sweeps(g, spans_a, spans_b, spans_q):
        numbers = par[pl.ds(pl.multiple_of(g * 8, 8), 8), :]
        om = jnp.broadcast_to(BASE_FREQ * numbers[:, 0:1], (8, WIDE))
        am = jnp.broadcast_to(numbers[:, 1:2], (8, WIDE))
        ct = jnp.broadcast_to(numbers[:, 2:3], (8, WIDE))
        mask = jnp.where(jnp.logical_and(block >= 0.0, block < ct), 1.0, 0.0)
        scale = 0.5 * (om * om) * (am * am) * mask

        def first_sweep(at, size, ok):
            con, cur = con_b[pl.ds(at, size)], cur_b[pl.ds(at, size)]
            product = om[None] * con
            inverse = 1.0 / (16.0 + product * product)
            re = inverse * (mask * (4.0 * ok))[None]
            im = product * (inverse * (mask * -ok)[None])
            inv_r[pl.ds(at, size)] = re
            inv_i[pl.ds(at, size)] = im
            a_r[pl.ds(at, size)] = cur * re
            a_i[pl.ds(at, size)] = cur * im
            weight[pl.ds(at, size)] = (scale[None] * con) * inverse

        def second_sweep(at, size):
            near_r = cur_b[pl.ds(at, size)] + neighbours(a_r, at, size)
            near_i = neighbours(a_i, at, size)
            re, im = inv_r[pl.ds(at, size)], inv_i[pl.ds(at, size)]
            b_r[pl.ds(at, size)] = near_r * re - near_i * im
            b_i[pl.ds(at, size)] = near_r * im + near_i * re

        def third_sweep(at, size):
            near_r = cur_b[pl.ds(at, size)] + neighbours(b_r, at, size)
            near_i = neighbours(b_i, at, size)
            loss = weight[pl.ds(at, size)] * (near_r * near_r + near_i * near_i)
            total[pl.ds(at, size)] = total[pl.ds(at, size)] + loss

        for span in spans_a:
            first_sweep(*span)
        for span in spans_b:
            second_sweep(*span)
        for span in spans_q:
            third_sweep(*span)

    end = PAD + ROWS

    def middle(g):
        sweeps(
            g,
            [(at, 4, 1.0) for at in range(PAD, end, 4)],
            [(at, 3) for at in range(PAD + 1, end - 1, 3)],
            [(at, 4) for at in range(PAD + 2, end - 2, 4)],
        )

    def rims(g):
        sweeps(
            g,
            [(3, 3, up_ok), (6, 2, up_ok), (8, 4, 1.0), (end - 4, 4, 1.0), (end, 2, down_ok), (end + 2, 3, down_ok)],
            [(4, 4), (8, 3), (end - 3, 4), (end + 1, 3)],
            [(5, 5), (end - 2, 5)],
        )

    def rows_of(g):
        def rows_here(at, size):
            rows = par.at[pl.ds(at, size)]
            pltpu.make_async_remote_copy(rows, rows, send_sem, recv_sem.at[g], below, MESH).wait_recv()

        @pl.when(low)
        def _():
            @pl.when(g == 0)
            def _():
                rows_here(1, 7)

            pl.when(g > 0)(lambda: rows_here(0, 8))

        @pl.when(jnp.logical_and(low, g == 3))
        def _():
            all_copy.start()

        @pl.when(jnp.logical_and(high, g == 0))
        def _():
            all_copy.wait_recv()


    def early(g, t):
        rows_of(g)
        middle(g)
        return t

    def early_rims(g, t):
        rims(g)
        return t

    def late(g, t):
        rows_of(g)
        middle(g)
        rims(g)
        return t

    def start_total(i, t):
        total[pl.ds(4 + 4 * i, 4)] = jnp.zeros((4, 8, WIDE), jnp.float32)
        return t

    lax.fori_loop(0, 10, start_total, 0)
    lift(range(PAD, end))

    ahead = jnp.where(low, 2, 0)
    lax.fori_loop(0, ahead, early, 0)

    to_below.wait_recv()

    @pl.when(z == 6)
    def _():
        to_above.start()

    row = lax.broadcasted_iota(jnp.int32, (TALL, WIDE), 0)
    col = lax.broadcasted_iota(jnp.int32, (TALL, WIDE), 1)
    in_grid = jnp.logical_and(
        jnp.logical_and(jnp.logical_or(row >= PAD, m > 0), jnp.logical_or(row < PAD + ROWS, m < SLABS - 1)),
        jnp.logical_and(
            jnp.logical_or(col < BLK + BLK // 2, h > 0),
            jnp.logical_or(jnp.logical_or(col < BLK, col >= BLK + BLK // 2), h < HARMS - 1),
        ),
    )
    rec[...] = jnp.where(in_grid, 1.0 / (4.0 + field[2]), 0.0)
    packed[...] = jnp.zeros_like(packed)
    lift([*range(3, PAD), *range(end, end + 5)])
    lax.fori_loop(0, ahead, early_rims, 0)
    lax.fori_loop(ahead, 4, late, 0)

    for r in range(5, TALL - 5):
        packed[r : r + 1, :] = jnp.sum(total[r], axis=0, keepdims=True)
    share = rec[...]
    mean = packed[...]
    warm = mean * share
    for sweep in range(3):
        warm = (
            mean
            + (pltpu.roll(warm, 1, 0) + pltpu.roll(warm, TALL - 1, 0))
            + (pltpu.roll(warm, 1, 1) + pltpu.roll(warm, WIDE - 1, 1))
        ) * share
    both[0] = mean[PAD : PAD + ROWS, 0:BLK]
    both[1] = warm[PAD : PAD + ROWS, 0:BLK]

    def rows_sent(size):
        rows = par.at[pl.ds(0, size)]
        pltpu.make_async_remote_copy(rows, rows, send_sem, recv_sem.at[0], below, MESH).wait_send()

    @pl.when(z != 5)
    def _():
        to_below.wait_send()

    @pl.when(z == 11)
    def _():
        to_zero.wait_send()


    @pl.when(z != 0)
    def _():
        to_above.wait_send()

    @pl.when(z == 6)
    def _():
        to_fifth.wait_send()

    @pl.when(high)
    def _():
        rows_sent(RING)

    @pl.when(low)
    def _():
        all_copy.wait_send()
        rows_sent(RING - 1)


def exchange_and_solve(current_pattern, conductivity, cooling, harm_order, harm_amp, block_counts):
    f32 = jnp.float32
    tall = pltpu.VMEM((TALL, 8, WIDE), f32)
    return pl.pallas_call(
        kernel,
        out_shape=jax.ShapeDtypeStruct((2, ROWS, BLK), f32),
        in_specs=[pl.BlockSpec(memory_space=pltpu.HBM)] * 3 + [pl.BlockSpec(memory_space=pltpu.SMEM)] * 3,
        out_specs=pl.BlockSpec(memory_space=pltpu.VMEM),
        scratch_shapes=[
            pltpu.VMEM((3, TALL, WIDE), f32),
            pltpu.VMEM((3, 3, ROWS, BLK), f32),
            pltpu.VMEM((3, PAD, WIDE), f32),
            pltpu.VMEM((3, 3, PAD, BLK), f32),
            pltpu.VMEM((1, BLK), f32),
            pltpu.VMEM((HARMS, BLK), f32),
            tall, tall, tall, tall, tall, tall, tall, tall, tall, tall,
            pltpu.VMEM((TALL, WIDE), f32),
            pltpu.VMEM((TALL, WIDE), f32),
            pltpu.SemaphoreType.DMA,
            pltpu.SemaphoreType.DMA,
            pltpu.SemaphoreType.DMA,
            pltpu.SemaphoreType.DMA((4,)),
            pltpu.SemaphoreType.DMA((3,)),
            pltpu.SemaphoreType.DMA((2,)),
            pltpu.SemaphoreType.DMA,
            pltpu.SemaphoreType.DMA,
        ],
        compiler_params=pltpu.CompilerParams(collective_id=0, has_side_effects=True),
    )(current_pattern, conductivity, cooling, harm_order, harm_amp, block_counts)


def on_device(*args):
    both = lax.cond(
        lax.axis_index("harm") < HARMS,
        exchange_and_solve,
        lambda *a: jnp.zeros((2, ROWS, BLK), jnp.float32),
        *args,
    )
    return both[0] * (1.0 / HARMS), both[1] * (1.0 / HARMS)


def solution(mesh):
    return jax.shard_map(
        on_device,
        mesh=mesh,
        in_specs=(
            P("mesh", None),
            P("mesh", None),
            P("mesh", None),
            P("harm"),
            P("harm"),
            P("harm"),
        ),
        out_specs=(P("mesh", "harm"), P("mesh", "harm")),
        check_vma=False,
    )
```

```python
import functools

import jax
import jax.numpy as jnp
from jax import lax
from jax.experimental import pallas as pl
from jax.experimental.pallas import tpu as pltpu
from jax.sharding import PartitionSpec as P

MESH = pl.DeviceIdType.MESH
BASE_FREQ = 0.1
HARMS = 32
SLABS = 24
ROWS = 32
BLK = 128
WIDE = 2 * BLK
PAD = 8
TALL = ROWS + 2 * PAD
RING = HARMS // 2


AROUND = tuple((dy, dc) for dy in (4, 5, 3, 6, 2, 7, 1, 0) for dc in (1, 0))


def steps_below(value, step, count):
    return sum((value >= step * k).astype(jnp.int32) for k in range(1, count))


def kernel(
    current, conductivity, cooling, order, amp, count, both,
    field, parts, other, other_parts, msg, par, cur_b, con_b, inv_r, inv_i, a_r, a_i, b_r, b_i, weight, total, packed, rec,
    load_sem, other_sem, send_sem, recv_sem, edge_send, edge_recv, all_send, all_recv,
):
    m, h = lax.axis_index("mesh"), lax.axis_index("harm")
    x, y = steps_below(m, 6, 4), steps_below(h, 4, 8)
    z_lo = m - 6 * x
    z_hi = (h - 4 * y >= 2).astype(jnp.int32)
    c = h - 4 * y - 2 * z_hi
    z = z_lo + 6 * z_hi
    low, high = z < 6, z >= 6
    last = z_lo == 5
    above = (jnp.where(m == 0, SLABS - 1, m - 1), h)
    below = (jnp.where(m == SLABS - 1, 0, m + 1), h)
    after = jnp.where(x == 3, m - 18, m + 6) - 5
    before = jnp.where(x == 0, m + 18, m - 6) + 5
    own_half = [2 * z_hi + c, 2 * z_hi + (1 - c)]
    other_half = [2 * (1 - z_hi) + c, 2 * (1 - z_hi) + (1 - c)]
    around_y = [4 * jnp.where(y + d >= 8, y + d - 8, y + d) for d in range(8)]
    low_move = jnp.where(z_lo == 0, 4, jnp.where(z_lo == 1, 2, jnp.where(z_lo == 2, 3, -3)))
    high_move = jnp.where(z_lo == 4, -4, jnp.where(z_lo == 3, -2, jnp.where(z_lo == 5, -3, 3)))
    mirror = m + jnp.where(low, low_move, high_move)

    def inside(dy, dc):
        return m, around_y[dy % 8] + own_half[dc]

    def across(dy, dc):
        return mirror, around_y[dy % 8] + other_half[dc]

    barrier = pltpu.get_barrier_semaphore()

    def greet(who):
        pl.semaphore_signal(barrier, inc=1, device_id=who, device_id_type=MESH)

    @pl.when(jnp.logical_not(last))
    def _():
        greet(below)

    @pl.when(z == 5)
    def _():
        greet((after, h + 2))

    @pl.when(z == 6)
    def _():
        greet(above)

    @pl.when(z == 0)
    def _():
        greet((before, h + 2))

    @pl.when(low)
    def _():
        for dy, dc in AROUND[:-1]:
            greet(inside(dy, dc))
        for dy, dc in AROUND:
            greet(across(dy, dc))

    left = jnp.maximum(h - 1, 0)
    right = jnp.minimum(h + 1, HARMS - 1)
    for i, source in enumerate((current, conductivity, cooling)):
        for j, block in enumerate((h, left, right)):
            columns = pl.ds(pl.multiple_of(block * BLK, BLK), BLK)
            pltpu.make_async_copy(source.at[:, columns], parts.at[i, j], load_sem).start()
    lends = jnp.logical_or(z == 6, z == 11)
    lent_rows = pl.ds(pl.multiple_of(jnp.where(z == 6, 0, ROWS - PAD), PAD), PAD)

    @pl.when(lends)
    def _():
        for i, source in enumerate((current, conductivity, cooling)):
            for j, block in enumerate((h - 2, jnp.maximum(h - 3, 0), h - 1)):
                columns = pl.ds(pl.multiple_of(block * BLK, BLK), BLK)
                pltpu.make_async_copy(source.at[lent_rows, columns], other_parts.at[i, j], other_sem).start()

    lane = lax.broadcasted_iota(jnp.int32, (1, BLK), 1)
    numbers = [jnp.full((1, BLK), v[0], jnp.int32) for v in (order, amp, count)]
    msg[...] = jnp.where(lane == 0, numbers[0], jnp.where(lane == 1, numbers[1], numbers[2])).astype(jnp.float32)

    links = jnp.where(z == 0, 0, 1) + jnp.where(z == 11, 2, 0)
    pl.semaphore_wait(barrier, links + jnp.where(low, 15, 16))

    def row_copy(i, crossing):
        dy, dc = AROUND[i]
        slot = RING * crossing + RING - 1 - i
        return pltpu.make_async_remote_copy(
            msg,
            par.at[pl.ds(slot, 1)],
            send_sem,
            recv_sem.at[slot // 8],
            (across if crossing else inside)(-dy, dc),
            MESH,
        )

    half = lax.broadcasted_iota(jnp.int32, (ROWS, BLK), 1) < BLK // 2
    to_fifth = pltpu.make_async_remote_copy(
        other,
        field.at[:, pl.ds(PAD + ROWS, PAD)],
        edge_send.at[2],
        edge_recv.at[1],
        (before, h - 2),
        MESH,
    )

    to_zero = pltpu.make_async_remote_copy(
        other, field.at[:, pl.ds(0, PAD)], edge_send.at[2], edge_recv.at[0], (after, h - 2), MESH
    )

    @pl.when(high)
    def _():
        for i in range(RING):
            row_copy(i, 1).start()

    @pl.when(low)
    def _():
        par[0:1, :] = msg[...]
        for i in range(RING - 1):
            row_copy(i, 0).start()

    @pl.when(lends)
    def _():
        pltpu.make_async_copy(other_parts, other_parts, other_sem).wait()
        for i in range(3):
            other[i, :, 0:BLK] = other_parts[i, 0]
            other[i, :, BLK:WIDE] = jnp.where(half[0:PAD], other_parts[i, 2], other_parts[i, 1])
        pl.when(z == 6)(to_fifth.start)
        pl.when(z == 11)(to_zero.start)

    pltpu.make_async_copy(parts, parts, load_sem).wait()
    for i in range(3):
        field[i, PAD : PAD + ROWS, 0:BLK] = parts[i, 0]
        field[i, PAD : PAD + ROWS, BLK:WIDE] = jnp.where(half, parts[i, 2], parts[i, 1])

    to_below = pltpu.make_async_remote_copy(
        field.at[:, pl.ds(ROWS, PAD)], field.at[:, pl.ds(0, PAD)], edge_send.at[0], edge_recv.at[0], below, MESH
    )
    to_above = pltpu.make_async_remote_copy(
        field.at[:, pl.ds(PAD, PAD)], field.at[:, pl.ds(PAD + ROWS, PAD)], edge_send.at[1], edge_recv.at[1], above, MESH
    )

    @pl.when(z_lo != 0)
    def _():
        to_above.start()

    @pl.when(z == 11)
    def _():
        to_below.start()

    to_above.wait_recv()

    @pl.when(jnp.logical_not(last))
    def _():
        to_below.start()

    ext_lane = lax.broadcasted_iota(jnp.int32, (8, WIDE), 1)
    block = jnp.where(ext_lane < BLK, h, jnp.where(ext_lane < BLK + BLK // 2, h + 1, h - 1)).astype(jnp.float32)
    up_ok = jnp.where(m > 0, 1.0, 0.0)
    down_ok = jnp.where(m < SLABS - 1, 1.0, 0.0)
    all_copy = pltpu.make_async_remote_copy(
        par, par, all_send, all_recv, across(0, 0), MESH
    )

    def neighbours(ref, at, size):
        mid = ref[pl.ds(at, size)]
        return (ref[pl.ds(at - 1, size)] + ref[pl.ds(at + 1, size)]) + (
            pltpu.roll(mid, 1, 2) + pltpu.roll(mid, WIDE - 1, 2)
        )

    def lift(rows):
        for r in rows:
            cur_b[r] = jnp.broadcast_to(field[0, r : r + 1, :], (8, WIDE))
            con_b[r] = jnp.broadcast_to(field[1, r : r + 1, :], (8, WIDE))

    def sweeps(g, spans_a, spans_b, spans_q):
        numbers = par[pl.ds(pl.multiple_of(g * 8, 8), 8), :]
        om = jnp.broadcast_to(BASE_FREQ * numbers[:, 0:1], (8, WIDE))
        am = jnp.broadcast_to(numbers[:, 1:2], (8, WIDE))
        ct = jnp.broadcast_to(numbers[:, 2:3], (8, WIDE))
        mask = jnp.where(jnp.logical_and(block >= 0.0, block < ct), 1.0, 0.0)
        scale = 0.5 * (om * om) * (am * am) * mask

        def first_sweep(at, size, ok):
            con, cur = con_b[pl.ds(at, size)], cur_b[pl.ds(at, size)]
            product = om[None] * con
            inverse = 1.0 / (16.0 + product * product)
            re = inverse * (mask * (4.0 * ok))[None]
            im = product * (inverse * (mask * -ok)[None])
            inv_r[pl.ds(at, size)] = re
            inv_i[pl.ds(at, size)] = im
            a_r[pl.ds(at, size)] = cur * re
            a_i[pl.ds(at, size)] = cur * im
            weight[pl.ds(at, size)] = (scale[None] * con) * inverse

        def second_sweep(at, size):
            near_r = cur_b[pl.ds(at, size)] + neighbours(a_r, at, size)
            near_i = neighbours(a_i, at, size)
            re, im = inv_r[pl.ds(at, size)], inv_i[pl.ds(at, size)]
            b_r[pl.ds(at, size)] = near_r * re - near_i * im
            b_i[pl.ds(at, size)] = near_r * im + near_i * re

        def third_sweep(at, size):
            near_r = cur_b[pl.ds(at, size)] + neighbours(b_r, at, size)
            near_i = neighbours(b_i, at, size)
            loss = weight[pl.ds(at, size)] * (near_r * near_r + near_i * near_i)
            total[pl.ds(at, size)] = total[pl.ds(at, size)] + loss

        for span in spans_a:
            first_sweep(*span)
        for span in spans_b:
            second_sweep(*span)
        for span in spans_q:
            third_sweep(*span)

    end = PAD + ROWS

    def middle(g):
        sweeps(
            g,
            [(at, 4, 1.0) for at in range(PAD, end, 4)],
            [(at, 3) for at in range(PAD + 1, end - 1, 3)],
            [(at, 4) for at in range(PAD + 2, end - 2, 4)],
        )

    def rims(g):
        sweeps(
            g,
            [(3, 3, up_ok), (6, 2, up_ok), (8, 4, 1.0), (end - 4, 4, 1.0), (end, 2, down_ok), (end + 2, 3, down_ok)],
            [(4, 4), (8, 3), (end - 3, 4), (end + 1, 3)],
            [(5, 5), (end - 2, 5)],
        )

    def rows_of(g):
        def rows_here(at, size):
            rows = par.at[pl.ds(at, size)]
            pltpu.make_async_remote_copy(rows, rows, send_sem, recv_sem.at[g], below, MESH).wait_recv()

        @pl.when(low)
        def _():
            @pl.when(g == 0)
            def _():
                rows_here(1, 7)

            pl.when(g > 0)(lambda: rows_here(0, 8))

        @pl.when(jnp.logical_and(low, g == 3))
        def _():
            all_copy.start()

        @pl.when(jnp.logical_and(high, g == 0))
        def _():
            all_copy.wait_recv()


    def early(g, t):
        rows_of(g)
        middle(g)
        return t

    def early_rims(g, t):
        rims(g)
        return t

    def late(g, t):
        rows_of(g)
        middle(g)
        rims(g)
        return t

    def start_total(i, t):
        total[pl.ds(4 + 4 * i, 4)] = jnp.zeros((4, 8, WIDE), jnp.float32)
        return t

    lax.fori_loop(0, 10, start_total, 0)
    lift(range(PAD, end))

    ahead = jnp.where(low, 2, 0)
    lax.fori_loop(0, ahead, early, 0)

    to_below.wait_recv()

    @pl.when(z == 6)
    def _():
        to_above.start()

    row = lax.broadcasted_iota(jnp.int32, (TALL, WIDE), 0)
    col = lax.broadcasted_iota(jnp.int32, (TALL, WIDE), 1)
    in_grid = jnp.logical_and(
        jnp.logical_and(jnp.logical_or(row >= PAD, m > 0), jnp.logical_or(row < PAD + ROWS, m < SLABS - 1)),
        jnp.logical_and(
            jnp.logical_or(col < BLK + BLK // 2, h > 0),
            jnp.logical_or(jnp.logical_or(col < BLK, col >= BLK + BLK // 2), h < HARMS - 1),
        ),
    )
    rec[...] = jnp.where(in_grid, 1.0 / (4.0 + field[2]), 0.0)
    packed[...] = jnp.zeros_like(packed)
    lift([*range(3, PAD), *range(end, end + 5)])
    lax.fori_loop(0, ahead, early_rims, 0)
    lax.fori_loop(ahead, 4, late, 0)

    for r in range(5, TALL - 5):
        packed[r : r + 1, :] = jnp.sum(total[r], axis=0, keepdims=True)
    share = rec[...]
    mean = packed[...]
    warm = mean * share
    for sweep in range(3):
        warm = (
            mean
            + (pltpu.roll(warm, 1, 0) + pltpu.roll(warm, TALL - 1, 0))
            + (pltpu.roll(warm, 1, 1) + pltpu.roll(warm, WIDE - 1, 1))
        ) * share
    both[0] = mean[PAD : PAD + ROWS, 0:BLK]
    both[1] = warm[PAD : PAD + ROWS, 0:BLK]

    def rows_sent(size):
        rows = par.at[pl.ds(0, size)]
        pltpu.make_async_remote_copy(rows, rows, send_sem, recv_sem.at[0], below, MESH).wait_send()

    @pl.when(z != 5)
    def _():
        to_below.wait_send()

    @pl.when(z == 11)
    def _():
        to_zero.wait_send()


    @pl.when(z != 0)
    def _():
        to_above.wait_send()

    @pl.when(z == 6)
    def _():
        to_fifth.wait_send()

    @pl.when(high)
    def _():
        rows_sent(RING)

    @pl.when(low)
    def _():
        all_copy.wait_send()
        rows_sent(RING - 1)


def exchange_and_solve(current_pattern, conductivity, cooling, harm_order, harm_amp, block_counts):
    f32 = jnp.float32
    tall = pltpu.VMEM((TALL, 8, WIDE), f32)
    return pl.pallas_call(
        kernel,
        out_shape=jax.ShapeDtypeStruct((2, ROWS, BLK), f32),
        in_specs=[pl.BlockSpec(memory_space=pltpu.HBM)] * 3 + [pl.BlockSpec(memory_space=pltpu.SMEM)] * 3,
        out_specs=pl.BlockSpec(memory_space=pltpu.VMEM),
        scratch_shapes=[
            pltpu.VMEM((3, TALL, WIDE), f32),
            pltpu.VMEM((3, 3, ROWS, BLK), f32),
            pltpu.VMEM((3, PAD, WIDE), f32),
            pltpu.VMEM((3, 3, PAD, BLK), f32),
            pltpu.VMEM((1, BLK), f32),
            pltpu.VMEM((HARMS, BLK), f32),
            tall, tall, tall, tall, tall, tall, tall, tall, tall, tall,
            pltpu.VMEM((TALL, WIDE), f32),
            pltpu.VMEM((TALL, WIDE), f32),
            pltpu.SemaphoreType.DMA,
            pltpu.SemaphoreType.DMA,
            pltpu.SemaphoreType.DMA,
            pltpu.SemaphoreType.DMA((4,)),
            pltpu.SemaphoreType.DMA((3,)),
            pltpu.SemaphoreType.DMA((2,)),
            pltpu.SemaphoreType.DMA,
            pltpu.SemaphoreType.DMA,
        ],
        compiler_params=pltpu.CompilerParams(collective_id=0, has_side_effects=True),
    )(current_pattern, conductivity, cooling, harm_order, harm_amp, block_counts)


def on_device(*args):
    both = lax.cond(
        lax.axis_index("harm") < HARMS,
        exchange_and_solve,
        lambda *a: jnp.zeros((2, ROWS, BLK), jnp.float32),
        *args,
    )
    return both[0] * (1.0 / HARMS), both[1] * (1.0 / HARMS)


def solution(mesh):
    return jax.shard_map(
        on_device,
        mesh=mesh,
        in_specs=(
            P("mesh", None),
            P("mesh", None),
            P("mesh", None),
            P("harm"),
            P("harm"),
            P("harm"),
        ),
        out_specs=(P("mesh", "harm"), P("mesh", "harm")),
        check_vma=False,
    )
```
